32 devices in a mesh: blk: 8 (over y, x, core), feat: 4 (over z).
Axes of the slice: x: 2, y: 2, z: 4, core: 2. Of those that a mesh axis runs over, the one named last changes fastest.
Arguments:
- features: bfloat16 [24576, 512], P('blk', 'feat'), may hold values from -6 to 6
- tile_values: bfloat16 [1024, 128, 128], P('blk'), may hold values from -0.375 to 0.375
- tile_rows: int32 [1024], P('blk'), may hold values from 0 to 23, as said below
- tile_cols: int32 [1024], P('blk'), may hold values from 0 to 23, as said below
- tile_counts: int32 [64], P('blk'), may hold values from 1 to 16, as said below
- weight: bfloat16 [512, 512], replicated, may hold values from -0.25 to 0.25
- bias: float32 [512], P('feat'), may hold values from -3 to 3
Outputs:
- hidden: bfloat16 [24576, 512], P('blk', 'feat')
The draws below stay inside these ranges and needn't reach their ends.
Inputs may be any that keep to these rules, and one draw needn't show every extreme that they name: `tile_rows`: the live slots of one node block and offset name distinct pairs of row and column tiles. `tile_cols`: paired with tile_rows slot by slot. `tile_counts`: some block and offset has all 16 slots live in every draw.
All inputs are finite; a program needn't handle non-finite values.
Results may differ from the reference program's by a relative error of at most 0.0049.
Values may be sent and summed in bfloat16 or wider, within the bound.
No kernel may reach another device: no remote copies, remote signals or barrier semaphores. Data moves between devices by JAX's collectives and lax.ppermute only.
A program may use at most 64 MiB of HBM per device.

```python
import jax
import jax.numpy as jnp
from jax import lax

F_IN = 512
F_OUT = 512
TILE = 128
STEPS = 8
MAXT = 16
RT_DEV = 24
ROWS = 24576
SLOTS = 1024
N_BLK = 8


def slot_pairs(key):
    base = jax.random.fold_in(key, 11)
    keys_all = jax.random.split(base, N_BLK * STEPS)
    orders = jax.vmap(lambda single: jax.random.permutation(single, RT_DEV * RT_DEV))(keys_all)
    return orders[:, :MAXT].reshape(N_BLK * STEPS * MAXT).astype(jnp.int32)


def draw_tile_rows(key, part):
    return (slot_pairs(key) // RT_DEV).astype(jnp.int32)


def draw_tile_cols(key, part):
    return (slot_pairs(key) % RT_DEV).astype(jnp.int32)


def draw_tile_counts(key, part):
    base = jax.random.fold_in(key, 23)
    first_key, second_key, third_key, fourth_key = jax.random.split(base, 4)
    levels = 2 ** jax.random.randint(first_key, (N_BLK, 1), 1, 4)
    ceiling = jnp.maximum(levels * MAXT // 8, 1)
    raw_counts = MAXT - jax.random.randint(second_key, (N_BLK, STEPS), 0, 1048576) % ceiling
    total_slots = N_BLK * STEPS
    chosen = jax.random.randint(third_key, (), 0, total_slots)
    other = (chosen + 1 + jax.random.randint(fourth_key, (), 0, total_slots - 1)) % total_slots
    flat_counts = raw_counts.reshape(total_slots)
    places = jnp.arange(total_slots)
    flat_counts = jnp.where(places == chosen, MAXT, flat_counts)
    flat_counts = jnp.where(places == other, 1, flat_counts)
    return flat_counts.astype(jnp.int32)


def block_scale(key, extent, pieces, low, top_value):
    factor_of = 1.0
    for dim, blocks in pieces:
        draws = jax.random.uniform(jax.random.fold_in(jax.random.fold_in(key, 6), dim), (blocks,), jnp.float32, low / len(pieces), top_value / len(pieces))
        factor_of = factor_of * jnp.repeat(jnp.exp(draws), extent[dim] // blocks).reshape((-1,) + (1,) * (len(extent) - 1 - dim))
    return factor_of


def gaussian(own_key, shape, scale, reach, pieces=(), kind=jnp.bfloat16):
    values = jax.random.normal(own_key, shape, jnp.float32) * scale
    if len(pieces) > 0:
        values = block_scale(own_key, shape, pieces, -0.22, 0.18) * values
    return jnp.clip(values, min=-reach, max=reach).astype(kind)


def setup_inputs(seed: int = 0) -> dict:
    keys = jax.random.split(jax.random.key(seed), 8)
    features = gaussian(keys[0], (ROWS, F_IN), 1.0, 6.0, ((0, 8), (1, 4)))
    tile_values = gaussian(keys[1], (SLOTS, TILE, TILE), (TILE * 2) ** -0.5, 0.375, ((0, 8),))
    tile_rows = draw_tile_rows(jax.random.fold_in(keys[7], 71), 0)
    tile_cols = draw_tile_cols(jax.random.fold_in(keys[7], 71), 0)
    tile_counts = draw_tile_counts(jax.random.fold_in(keys[7], 71), 0)
    weight = gaussian(keys[5], (F_IN, F_OUT), F_IN ** -0.5, 0.25)
    bias = gaussian(keys[6], (F_OUT,), 0.5, 3.0, ((0, 4),), jnp.float32)
    return {"features": features, "tile_values": tile_values, "tile_rows": tile_rows, "tile_cols": tile_cols, "tile_counts": tile_counts, "weight": weight, "bias": bias}


def reference(features, tile_values, tile_rows, tile_cols, tile_counts, weight, bias):
    blocks = features.reshape(N_BLK, RT_DEV, TILE, F_IN)
    values_all = tile_values.reshape(N_BLK, STEPS, MAXT, TILE, TILE)
    row_ids = tile_rows.reshape(N_BLK, STEPS, MAXT)
    col_ids = tile_cols.reshape(N_BLK, STEPS, MAXT)
    counts_all = tile_counts.reshape(N_BLK, STEPS)

    def one_block(index):
        totals = jnp.zeros((RT_DEV, TILE, F_IN), jnp.float32)
        for offset in range(STEPS):
            source = blocks[(index - offset) % N_BLK]
            picked = jnp.take(source, col_ids[index, offset], axis=0).astype(jnp.float32)
            products = jnp.einsum("ktj,kjf->ktf", values_all[index, offset].astype(jnp.float32), picked, precision=lax.Precision.HIGHEST)
            active = jnp.arange(MAXT, dtype=jnp.int32) < counts_all[index, offset]
            one_hot = ((row_ids[index, offset][None, :] == jnp.arange(RT_DEV, dtype=jnp.int32)[:, None]) & active[None, :]).astype(jnp.float32)
            totals = totals + jnp.einsum("rk,ktf->rtf", one_hot, products, precision=lax.Precision.HIGHEST)
        aggregate = totals.reshape(RT_DEV * TILE, F_IN).astype(jnp.bfloat16)
        mixed = jnp.dot(aggregate, weight, preferred_element_type=jnp.float32) + bias[None, :]
        return jnp.maximum(mixed, 0.0).astype(jnp.bfloat16)

    result = lax.map(one_block, jnp.arange(N_BLK, dtype=jnp.int32))
    return result.reshape(N_BLK * RT_DEV * TILE, F_OUT)
```

```python
import functools

import jax
import jax.numpy as jnp
from jax import lax
from jax.experimental import pallas as pl
from jax.experimental.pallas import tpu as pltpu
from jax.sharding import PartitionSpec as P

CHUNKS = (8, 8, 8)
UNROLL = 16


def shifted(shard, axis, by):
    count = lax.axis_size(axis)
    return lax.ppermute(shard, axis, [(i, (i + by) % count) for i in range(count)])


def flipped(shard, axis, bits):
    count = lax.axis_size(axis)
    return lax.ppermute(shard, axis, [(i, i ^ bits) for i in range(count)])


def pick_tiles(current, wanted, row_tiles, tile_size):
    source = current.reshape(row_tiles, tile_size, current.shape[-1])
    return jnp.take(source, wanted, axis=0)


def add_tiles(totals, picked, offset, values_all, row_ids, tile_counts):
    row_tiles = totals.shape[0]
    slot_count = row_ids.shape[1]
    products = jnp.einsum(
        "ktj,kjf->ktf", values_all[offset], picked, preferred_element_type=jnp.float32
    )
    active = jnp.arange(slot_count) < tile_counts[offset]
    one_hot = (
        (row_ids[offset][None, :] == jnp.arange(row_tiles)[:, None]) & active[None, :]
    ).astype(jnp.float32)
    return totals + jnp.einsum("rk,ktf->rtf", one_hot, products, precision=lax.Precision.HIGHEST)


def ring_body(features, tile_values, tile_rows, tile_cols, tile_counts, weight, bias):
    row_count, col_width = features.shape
    tile_size = tile_values.shape[-1]
    row_tiles = row_count // tile_size
    steps_all = tile_counts.shape[0]
    slot_count = tile_rows.shape[0] // steps_all
    values_all = tile_values.reshape(steps_all, slot_count, tile_size, tile_size)
    row_ids = tile_rows.reshape(steps_all, slot_count)
    col_ids = tile_cols.reshape(steps_all, slot_count)
    totals = jnp.zeros((row_tiles, tile_size, col_width), jnp.float32)
    own_picked = pick_tiles(features, col_ids[0], row_tiles, tile_size)
    totals = add_tiles(totals, own_picked, 0, values_all, row_ids, tile_counts)
    current = features
    for offset in range(1, steps_all):
        current = shifted(current, "blk", 1)
        picked = pick_tiles(current, col_ids[offset], row_tiles, tile_size)
        totals = add_tiles(totals, picked, offset, values_all, row_ids, tile_counts)
    aggregate = totals.reshape(row_count, col_width).astype(jnp.bfloat16)
    out_width = bias.shape[0]
    member = lax.axis_index("feat")
    own_cols = lax.dynamic_slice_in_dim(weight, member * out_width, out_width, 1)
    mixed = jnp.dot(
        lax.all_gather(aggregate, "feat", axis=1, tiled=True),
        own_cols,
        preferred_element_type=jnp.float32,
    )
    return jnp.maximum(mixed + bias[None, :], 0.0).astype(jnp.bfloat16)


def plan_kernel(edges, row_tiles, rows, cols, counts, place, order):
    steps = counts.shape[0]
    slots = rows.shape[0] // steps
    where = place[0]
    for part in range(len(edges) - 1):
        low, high = edges[part], edges[part + 1]

        def offset_loop(offset, found):
            source = where ^ ((where + steps - offset) & (steps - 1))

            def slot_loop(k, found):
                slot = offset * slots + k
                col = cols[slot]
                order[part, 0, found] = slot
                order[part, 1, found] = rows[slot]
                order[part, 2, found] = source * (high - low) + col - low
                return found + ((col >= low) & (col < high)).astype(jnp.int32)

            return lax.fori_loop(0, counts[offset], slot_loop, found)

        found = lax.fori_loop(0, steps, offset_loop, 0)
        for u in range(UNROLL):
            order[part, 0, found + u] = 0
            order[part, 1, found + u] = row_tiles
            order[part, 2, found + u] = 0
        order[part, 3, 0] = (found + UNROLL - 1) // UNROLL


def plan(edges, row_tiles, rows, cols, counts, place):
    parts = len(edges) - 1
    room = rows.shape[0] + UNROLL
    return pl.pallas_call(
        functools.partial(plan_kernel, edges, row_tiles),
        out_shape=jax.ShapeDtypeStruct((parts, 4, room), jnp.int32),
        in_specs=[pl.BlockSpec(memory_space=pltpu.SMEM)] * 4,
        out_specs=pl.BlockSpec(memory_space=pltpu.SMEM),
        name="plan",
    )(rows, cols, counts, place)


def mix_kernel(own, pair, across, far, weights, mine, other):
    width = own.shape[1]
    total = jnp.dot(own[...], weights[0], preferred_element_type=jnp.float32)
    for index, piece in enumerate((pair, across, far)):
        total += jnp.dot(piece[...], weights[index + 1], preferred_element_type=jnp.float32)
    mine[...] = total[:, :width].astype(mine.dtype)
    other[...] = total[:, width:].astype(other.dtype)


def mix(own, pair, across, far, weights):
    shape = jax.ShapeDtypeStruct(own.shape, own.dtype)
    return pl.pallas_call(
        mix_kernel,
        out_shape=(shape, shape),
        in_specs=[pl.BlockSpec(memory_space=pltpu.VMEM)] * 5,
        out_specs=(pl.BlockSpec(memory_space=pltpu.VMEM),) * 2,
        compiler_params=pltpu.CompilerParams(vmem_limit_bytes=16 << 20),
        cost_estimate=pl.CostEstimate(
            flops=16 * own.size * own.shape[1], bytes_accessed=12 * own.size, transcendentals=0
        ),
        name="mix",
    )(own, pair, across, far, weights)


def add_kernel(part, first, last, order, values, bias, *rest):
    pieces = rest[:8]
    rest = rest[8:]
    totals_in = None
    if not first:
        totals_in, rest = rest[0], rest[1:]
    out, held, sem, rest = rest[0], rest[1], rest[2], rest[3:]
    copies = []
    for index, piece in enumerate(pieces):
        size = piece.shape[0]
        copies.append(
            pltpu.make_async_copy(piece, held.at[pl.ds(index * size, size)], sem.at[index])
        )
        copies[-1].start()
    totals = rest[0] if last else out
    if first:
        totals[...] = jnp.zeros_like(totals)
    elif last:
        totals[...] = totals_in[...]
    for copy in copies:
        copy.wait()

    def group(g, carry):
        sums = []
        for u in range(UNROLL):
            index = g * UNROLL + u
            product = jnp.dot(
                values[order[part, 0, index]],
                held[order[part, 2, index]],
                preferred_element_type=jnp.float32,
            )
            sums.append((order[part, 1, index], product))
        for row, product in sums:
            totals[row] += product
        return carry

    lax.fori_loop(0, order[part, 3, 0], group, 0)
    if last:
        count = out.shape[0]

        def finish(r, carry):
            out[r] = jnp.maximum(totals[r] + bias[...], 0.0).astype(out.dtype)
            return carry

        lax.fori_loop(0, count, finish, 0)


def add_part(part, last, row_tiles, order, values, bias, pieces, totals):
    tile = values.shape[-1]
    width = pieces[0].shape[-1]
    first = totals is None
    size = pieces[0].shape[0]
    vmem = pl.BlockSpec(memory_space=pltpu.VMEM)
    any_space = pl.BlockSpec(memory_space=pl.ANY)
    operands = [order, values, bias, *pieces] + ([] if first else [totals])
    specs = [pl.BlockSpec(memory_space=pltpu.SMEM), vmem, vmem] + [any_space] * 8
    specs += [] if first else [vmem]
    total_shape = (row_tiles + 1, tile, width)
    scratch = [pltpu.VMEM((8 * size, tile, width), jnp.bfloat16), pltpu.SemaphoreType.DMA((8,))]
    if last:
        out_shape = jax.ShapeDtypeStruct((row_tiles, tile, width), jnp.bfloat16)
        scratch.append(pltpu.VMEM(total_shape, jnp.float32))
    else:
        out_shape = jax.ShapeDtypeStruct(total_shape, jnp.float32)
    return pl.pallas_call(
        functools.partial(add_kernel, part, first, last),
        out_shape=out_shape,
        in_specs=specs,
        out_specs=vmem,
        scratch_shapes=scratch,
        input_output_aliases={} if first or last else {len(operands) - 1: 0},
        compiler_params=pltpu.CompilerParams(vmem_limit_bytes=24 << 20),
        cost_estimate=pl.CostEstimate(
            flops=10**9, bytes_accessed=8 << 20, transcendentals=0
        ),
        name="add_tiles",
    )(*operands)


def body(features, tile_values, tile_rows, tile_cols, tile_counts, weight, bias):
    row_count, width = features.shape
    tile = tile_values.shape[-1]
    row_tiles = row_count // tile
    members = lax.axis_size("feat")
    member = lax.axis_index("feat")
    place = lax.axis_index("blk").reshape(1).astype(jnp.int32)
    edges = [0]
    for count in CHUNKS:
        edges.append(edges[-1] + count)
    order = plan(tuple(edges), row_tiles, tile_rows, tile_cols, tile_counts, place)
    blocks = weight.reshape(members, width, members, width)
    along = member ^ jnp.array([0, 1, 3, 2])
    across = member ^ jnp.array([0, 1])
    weights = blocks[along][:, :, across].reshape(members, width, 2 * width)
    middle = (member == 1) | (member == 2)
    inward, inner, outward = [(0, 1), (3, 2)], [(1, 2), (2, 1)], [(1, 0), (2, 3)]
    totals = None
    for part in range(len(edges) - 1):
        own = features[edges[part] * tile : edges[part + 1] * tile]
        pair = lax.ppermute(own, "feat", inward)
        opposite = lax.ppermute(own, "feat", inner)
        far = lax.ppermute(pair, "feat", inner)
        mine, other = mix(own, pair, opposite, far, weights)
        given = lax.ppermute(other, "feat", outward)
        mixed = jnp.where(middle, mine, given)
        beside = flipped(mixed, "blk", 2)
        above = flipped(mixed, "blk", 4)
        if part % 2 == 0:
            corner = flipped(beside, "blk", 4)
        else:
            corner = flipped(above, "blk", 2)
        pieces = []
        for piece in (mixed, beside, above, corner):
            pieces += [piece, flipped(piece, "blk", 1)]
        pieces = [piece.reshape(-1, tile, width) for piece in pieces]
        last = part == len(edges) - 2
        totals = add_part(part, last, row_tiles, order, tile_values, bias[None], pieces, totals)
    return totals.reshape(row_count, width)


def solution(mesh):
    in_specs = (
        P("blk", "feat"),
        P("blk", None, None),
        P("blk"),
        P("blk"),
        P("blk"),
        P(),
        P("feat"),
    )
    out_specs = P("blk", "feat")
    chosen = body if mesh.shape["blk"] == 8 and mesh.shape["feat"] == 4 else ring_body
    return jax.shard_map(chosen, mesh=mesh, in_specs=in_specs, out_specs=out_specs, check_vma=False)
```

```python
import functools

import jax
import jax.numpy as jnp
import numpy as np
from jax import lax
from jax.experimental import pallas as pl
from jax.experimental.pallas import tpu as pltpu
from jax.sharding import PartitionSpec as P

SPANS = (8, 8, 8)
FORWARD = (True, True, False)
UNROLL = 16


def shifted(shard, axis, by):
    count = lax.axis_size(axis)
    return lax.ppermute(shard, axis, [(i, (i + by) % count) for i in range(count)])


def flipped(shard, axis, bits):
    count = lax.axis_size(axis)
    return lax.ppermute(shard, axis, [(i, i ^ bits) for i in range(count)])


def pick_tiles(current, wanted, row_tiles, tile_size):
    source = current.reshape(row_tiles, tile_size, current.shape[-1])
    return jnp.take(source, wanted, axis=0)


def add_tiles(totals, picked, offset, values_all, row_ids, tile_counts):
    row_tiles = totals.shape[0]
    slot_count = row_ids.shape[1]
    products = jnp.einsum(
        "ktj,kjf->ktf", values_all[offset], picked, preferred_element_type=jnp.float32
    )
    active = jnp.arange(slot_count) < tile_counts[offset]
    one_hot = (
        (row_ids[offset][None, :] == jnp.arange(row_tiles)[:, None]) & active[None, :]
    ).astype(jnp.float32)
    return totals + jnp.einsum("rk,ktf->rtf", one_hot, products, precision=lax.Precision.HIGHEST)


def ring_body(features, tile_values, tile_rows, tile_cols, tile_counts, weight, bias):
    row_count, col_width = features.shape
    tile_size = tile_values.shape[-1]
    row_tiles = row_count // tile_size
    steps_all = tile_counts.shape[0]
    slot_count = tile_rows.shape[0] // steps_all
    values_all = tile_values.reshape(steps_all, slot_count, tile_size, tile_size)
    row_ids = tile_rows.reshape(steps_all, slot_count)
    col_ids = tile_cols.reshape(steps_all, slot_count)
    totals = jnp.zeros((row_tiles, tile_size, col_width), jnp.float32)
    own_picked = pick_tiles(features, col_ids[0], row_tiles, tile_size)
    totals = add_tiles(totals, own_picked, 0, values_all, row_ids, tile_counts)
    current = features
    for offset in range(1, steps_all):
        current = shifted(current, "blk", 1)
        picked = pick_tiles(current, col_ids[offset], row_tiles, tile_size)
        totals = add_tiles(totals, picked, offset, values_all, row_ids, tile_counts)
    aggregate = totals.reshape(row_count, col_width).astype(jnp.bfloat16)
    out_width = bias.shape[0]
    member = lax.axis_index("feat")
    own_cols = lax.dynamic_slice_in_dim(weight, member * out_width, out_width, 1)
    mixed = jnp.dot(
        lax.all_gather(aggregate, "feat", axis=1, tiled=True),
        own_cols,
        preferred_element_type=jnp.float32,
    )
    return jnp.maximum(mixed + bias[None, :], 0.0).astype(jnp.bfloat16)


def layouts():
    starts, sides = [], []
    for k, span in enumerate(SPANS):
        reach = span + (SPANS[k - 1] // 2 if k and FORWARD[k - 1] else 0)
        begin = [0, span, span + reach]
        side = span + 2 * reach
        if not FORWARD[k]:
            begin.append(side)
            side += span
        starts.append(begin)
        sides.append(side)
    return starts, sides


def spots():
    starts, sides = layouts()
    edges = np.cumsum((0,) + SPANS)
    table = np.zeros((8, int(edges[-1])), np.int32)
    for away in range(8):
        for k, span in enumerate(SPANS):
            for local in range(span):
                group, spot = k, local
                if away >> 1 < 3:
                    spot = starts[k][away >> 1] + local
                elif not FORWARD[k]:
                    spot = starts[k][3] + local
                else:
                    group = k + 1
                    piece = 1 if local < span // 2 else 2
                    spot = starts[group][piece] + SPANS[group] + local % (span // 2)
                table[away, edges[k] + local] = group * 1024 + (away & 1) * sides[group] + spot
    return table.reshape(-1)


def plan_kernel(row_tiles, rows, cols, counts, place, table, order, found):
    steps = counts.shape[0]
    slots = rows.shape[0] // steps
    where = place[0]
    for group in range(len(SPANS)):
        found[group] = 0

    def offset_loop(offset, carry):
        away = where ^ ((where + steps - offset) & (steps - 1))

        def slot_loop(k, carry):
            slot = offset * slots + k
            key = table[away * row_tiles + cols[slot]]
            group = key >> 10
            at = found[group]
            order[group, 0, at] = slot
            order[group, 1, at] = rows[slot]
            order[group, 2, at] = key & 1023
            found[group] = at + 1
            return carry

        return lax.fori_loop(0, counts[offset], slot_loop, carry)

    lax.fori_loop(0, steps, offset_loop, 0)
    for group in range(len(SPANS)):
        at = found[group]
        for u in range(UNROLL):
            order[group, 0, at + u] = 0
            order[group, 1, at + u] = row_tiles
            order[group, 2, at + u] = 0
        order[group, 3, 0] = (at + UNROLL - 1) // UNROLL


def plan(row_tiles, rows, cols, counts, place):
    room = rows.shape[0] + UNROLL
    return pl.pallas_call(
        functools.partial(plan_kernel, row_tiles),
        out_shape=jax.ShapeDtypeStruct((len(SPANS), 4, room), jnp.int32),
        in_specs=[pl.BlockSpec(memory_space=pltpu.SMEM)] * 5,
        out_specs=pl.BlockSpec(memory_space=pltpu.SMEM),
        scratch_shapes=[pltpu.SMEM((len(SPANS),), jnp.int32)],
        cost_estimate=pl.CostEstimate(flops=1000000000, bytes_accessed=1000, transcendentals=0),
        name="plan",
    )(rows, cols, counts, place, jnp.asarray(spots()))


def mix_kernel(members, count, member, own, pair, *rest):
    *received, weight, _, mine, other = rest
    width = own.shape[1]
    pieces = [own[...], pair[...]]
    for piece in received:
        pieces += [piece[k * count : (k + 1) * count] for k in range(piece.shape[0] // count)]
    me = member[0]

    def block(row, col):
        row = pl.multiple_of(row * width, width)
        col = pl.multiple_of(col * width, width)
        return weight[pl.ds(row, width), pl.ds(col, width)]

    rows = [me, me ^ 1, me ^ 3, me ^ 2]
    sides = [
        jnp.concatenate([block(row, me), block(row, me ^ 1)], axis=1) for row in rows
    ]
    total = jnp.dot(
        jnp.concatenate(pieces, axis=1),
        jnp.concatenate(sides, axis=0),
        preferred_element_type=jnp.float32,
    )
    mine[...] = total[:, :width].astype(mine.dtype)
    other[...] = total[:, width:].astype(other.dtype)


def mix(member, own, pair, received, weight, event):
    shape = jax.ShapeDtypeStruct(own.shape, own.dtype)
    vmem = pl.BlockSpec(memory_space=pltpu.VMEM)
    return pl.pallas_call(
        functools.partial(mix_kernel, 4, own.shape[0]),
        out_shape=(shape, shape),
        in_specs=[pl.BlockSpec(memory_space=pltpu.SMEM)]
        + [vmem] * (3 + len(received))
        + [pl.BlockSpec(memory_space=pl.ANY)],
        out_specs=(vmem, vmem),
        compiler_params=pltpu.CompilerParams(vmem_limit_bytes=16 << 20),
        cost_estimate=pl.CostEstimate(flops=1000, bytes_accessed=1000, transcendentals=0),
        name="mix",
    )(member, own, pair, *received, weight, event)


def add_kernel(group, first, last, starts, order, values, bias, *rest):
    pieces = rest[: len(starts)]
    rest = rest[len(starts) :]
    if not first:
        rest = rest[1:]
    if last:
        out, rest = rest[0], rest[1:]
    totals, token, held, sem = rest
    token[...] = jnp.zeros_like(token)
    copies = []
    for index, piece in enumerate(pieces):
        spot = held.at[pl.ds(starts[index], piece.shape[0])]
        copies.append(pltpu.make_async_copy(piece, spot, sem.at[index]))
        copies[-1].start()
    if first:
        totals[...] = jnp.zeros_like(totals)
    for copy in copies:
        copy.wait()

    def add(g, carry):
        sums = []
        for u in range(UNROLL):
            index = g * UNROLL + u
            product = jnp.dot(
                values[order[group, 0, index]],
                held[order[group, 2, index]],
                preferred_element_type=jnp.float32,
            )
            sums.append((order[group, 1, index], product))
        for row, product in sums:
            totals[row] += product
        return carry

    lax.fori_loop(0, order[group, 3, 0], add, 0)
    if last:

        def finish(r, carry):
            out[r] = jnp.maximum(totals[r] + bias[...], 0.0).astype(out.dtype)
            return carry

        lax.fori_loop(0, out.shape[0], finish, 0)


def add_group(group, row_tiles, order, values, bias, pieces, totals):
    tile = values.shape[-1]
    pieces = [piece.reshape(-1, tile, piece.shape[-1]) for piece in pieces]
    width = pieces[0].shape[-1]
    starts, sides = layouts()
    side = sides[group]
    starts = tuple(starts[group]) + tuple(start + side for start in starts[group])
    first, last = group == 0, group == len(SPANS) - 1
    vmem = pl.BlockSpec(memory_space=pltpu.VMEM)
    any_space = pl.BlockSpec(memory_space=pl.ANY)
    operands = [order, values, bias, *pieces] + ([] if first else [totals])
    specs = [pl.BlockSpec(memory_space=pltpu.SMEM), vmem, vmem] + [any_space] * len(pieces)
    specs += [] if first else [vmem]
    shapes = [
        jax.ShapeDtypeStruct((row_tiles + 1, tile, width), jnp.float32),
        jax.ShapeDtypeStruct((8, width), jnp.float32),
    ]
    if last:
        shapes = [jax.ShapeDtypeStruct((row_tiles, tile, width), jnp.bfloat16)] + shapes
    return pl.pallas_call(
        functools.partial(add_kernel, group, first, last, starts),
        out_shape=tuple(shapes),
        in_specs=specs,
        out_specs=(vmem,) * len(shapes),
        scratch_shapes=[
            pltpu.VMEM((2 * side, tile, width), jnp.bfloat16),
            pltpu.SemaphoreType.DMA((len(pieces),)),
        ],
        input_output_aliases={} if first else {len(operands) - 1: int(last)},
        compiler_params=pltpu.CompilerParams(vmem_limit_bytes=24 << 20),
        cost_estimate=pl.CostEstimate(flops=15000000000, bytes_accessed=1000, transcendentals=0),
        name="add_tiles",
    )(*operands)


def swap_inner(shard):
    blocks, members = lax.axis_size("blk"), lax.axis_size("feat")
    pairs = []
    for block in range(blocks):
        for member in range(members):
            if member in (1, 2):
                target = block * members + 3 - member
            else:
                target = (block ^ 1) * members + member
            pairs.append((block * members + member, target))
    return lax.ppermute(shard, ("blk", "feat"), pairs)


def swap_outer(shard):
    return lax.ppermute(shard, "feat", [(0, 1), (1, 0), (2, 3), (3, 2)])


def body(features, tile_values, tile_rows, tile_cols, tile_counts, weight, bias):
    row_count, width = features.shape
    tile = tile_values.shape[-1]
    row_tiles = row_count // tile
    member = lax.axis_index("feat").reshape(1).astype(jnp.int32)
    place = lax.axis_index("blk").reshape(1).astype(jnp.int32)
    middle = (member[0] == 1) | (member[0] == 2)
    count = len(SPANS)
    edges = [int(edge) * tile for edge in np.cumsum((0,) + SPANS)]
    order = plan(row_tiles, tile_rows, tile_cols, tile_counts, place)
    own = [features[edges[k] : edges[k + 1]] for k in range(count)]
    pairs = [swap_outer(own[0])]
    first = [swap_inner(own[0])]
    pairs.append(swap_outer(own[1]))
    later = swap_outer(features[edges[2] :])
    for k in range(2, count):
        pairs.append(later[edges[k] - edges[2] : edges[k + 1] - edges[2]])
    first.append(swap_inner(pairs[0]))
    received = [first]
    for k in range(1, count):
        received.append([swap_inner(jnp.concatenate([own[k], pairs[k]]))])
    totals = None
    events = [None] * (count + 2)
    steps = []
    for k in range(count):
        mine, other = mix(member, own[k], pairs[k], received[k], weight, order)
        mixed = jnp.where(middle, mine, swap_outer(other))
        to_beside = to_above = mixed
        if k and FORWARD[k - 1]:
            half = SPANS[k - 1] * tile // 2
            _, beside, above = steps[k - 1][:3]
            to_beside = jnp.concatenate([mixed, above[:half]])
            to_above = jnp.concatenate([mixed, beside[half : 2 * half]])
        step = [mixed, flipped(to_beside, "blk", 2), flipped(to_above, "blk", 4)]
        if not FORWARD[k]:
            step.append(flipped(mixed, "blk", 6))
        steps.append(step)
        pieces = step + [flipped(piece, "blk", 1) for piece in step]
        *out, totals, event = add_group(
            k, row_tiles, order, tile_values, bias[None], pieces, totals
        )
        events[k + 2] = event
    return out[0].reshape(row_count, width)


def solution(mesh):
    in_specs = (
        P("blk", "feat"),
        P("blk", None, None),
        P("blk"),
        P("blk"),
        P("blk"),
        P(),
        P("feat"),
    )
    out_specs = P("blk", "feat")
    chosen = body if mesh.shape["blk"] == 8 and mesh.shape["feat"] == 4 else ring_body
    return jax.shard_map(chosen, mesh=mesh, in_specs=in_specs, out_specs=out_specs, check_vma=False)
```

```python
import functools

import jax
import jax.numpy as jnp
import numpy as np
from jax import lax
from jax.experimental import pallas as pl
from jax.experimental.pallas import tpu as pltpu
from jax.sharding import PartitionSpec as P

CHUNKS = 2
UNROLL = 16
TURNS = (2, 3, 1)


def shifted(shard, axis, by):
    count = lax.axis_size(axis)
    return lax.ppermute(shard, axis, [(i, (i + by) % count) for i in range(count)])


def flipped(shard, axis, bits):
    count = lax.axis_size(axis)
    return lax.ppermute(shard, axis, [(i, i ^ bits) for i in range(count)])


def pick_tiles(current, wanted, row_tiles, tile_size):
    source = current.reshape(row_tiles, tile_size, current.shape[-1])
    return jnp.take(source, wanted, axis=0)


def add_tiles(totals, picked, offset, values_all, row_ids, tile_counts):
    row_tiles = totals.shape[0]
    slot_count = row_ids.shape[1]
    products = jnp.einsum(
        "ktj,kjf->ktf", values_all[offset], picked, preferred_element_type=jnp.float32
    )
    active = jnp.arange(slot_count) < tile_counts[offset]
    one_hot = (
        (row_ids[offset][None, :] == jnp.arange(row_tiles)[:, None]) & active[None, :]
    ).astype(jnp.float32)
    return totals + jnp.einsum("rk,ktf->rtf", one_hot, products, precision=lax.Precision.HIGHEST)


def ring_body(features, tile_values, tile_rows, tile_cols, tile_counts, weight, bias):
    row_count, col_width = features.shape
    tile_size = tile_values.shape[-1]
    row_tiles = row_count // tile_size
    steps_all = tile_counts.shape[0]
    slot_count = tile_rows.shape[0] // steps_all
    values_all = tile_values.reshape(steps_all, slot_count, tile_size, tile_size)
    row_ids = tile_rows.reshape(steps_all, slot_count)
    col_ids = tile_cols.reshape(steps_all, slot_count)
    totals = jnp.zeros((row_tiles, tile_size, col_width), jnp.float32)
    own_picked = pick_tiles(features, col_ids[0], row_tiles, tile_size)
    totals = add_tiles(totals, own_picked, 0, values_all, row_ids, tile_counts)
    current = features
    for offset in range(1, steps_all):
        current = shifted(current, "blk", 1)
        picked = pick_tiles(current, col_ids[offset], row_tiles, tile_size)
        totals = add_tiles(totals, picked, offset, values_all, row_ids, tile_counts)
    aggregate = totals.reshape(row_count, col_width).astype(jnp.bfloat16)
    out_width = bias.shape[0]
    member = lax.axis_index("feat")
    own_cols = lax.dynamic_slice_in_dim(weight, member * out_width, out_width, 1)
    mixed = jnp.dot(
        lax.all_gather(aggregate, "feat", axis=1, tiled=True),
        own_cols,
        preferred_element_type=jnp.float32,
    )
    return jnp.maximum(mixed + bias[None, :], 0.0).astype(jnp.bfloat16)


def tie(*arrays):
    return lax.optimization_barrier(arrays)


def spots(row_tiles):
    table = np.zeros((8, row_tiles), np.int32)
    for away in range(8):
        side, way = away & 1, away >> 1
        group = (0, 1, 1, 2)[way]
        start = (side, 2 * side, 2 * side + 1, side)[way] * row_tiles
        table[away] = group * 1024 + start + np.arange(row_tiles)
    return table.reshape(-1)


def plan_kernel(row_tiles, rows, cols, counts, place, table, order, found):
    steps = counts.shape[0]
    slots = rows.shape[0] // steps
    where = place[0]
    for group in range(3):
        found[group] = 0

    def offset_loop(offset, carry):
        away = where ^ ((where + steps - offset) & (steps - 1))

        def slot_loop(k, carry):
            slot = offset * slots + k
            key = table[away * row_tiles + cols[slot]]
            group = key >> 10
            at = found[group]
            order[group, 0, at] = slot
            order[group, 1, at] = rows[slot]
            order[group, 2, at] = key & 1023
            found[group] = at + 1
            return carry

        return lax.fori_loop(0, counts[offset], slot_loop, carry)

    lax.fori_loop(0, steps, offset_loop, 0)
    for group in range(3):
        at = found[group]
        for u in range(UNROLL):
            order[group, 0, at + u] = 0
            order[group, 1, at + u] = row_tiles
            order[group, 2, at + u] = 0
        order[group, 3, 0] = (at + UNROLL - 1) // UNROLL


def plan(row_tiles, rows, cols, counts, place):
    room = rows.shape[0] + UNROLL
    return pl.pallas_call(
        functools.partial(plan_kernel, row_tiles),
        out_shape=jax.ShapeDtypeStruct((3, 4, room), jnp.int32),
        in_specs=[pl.BlockSpec(memory_space=pltpu.SMEM)] * 5,
        out_specs=pl.BlockSpec(memory_space=pltpu.SMEM),
        scratch_shapes=[pltpu.SMEM((3,), jnp.int32)],
        cost_estimate=pl.CostEstimate(flops=10**9, bytes_accessed=1000, transcendentals=0),
        name="plan",
    )(rows, cols, counts, place, jnp.asarray(spots(row_tiles)))


def add_kernel(group, first, last, count, order, member, values, *rest):
    pieces, rest = rest[:count], rest[count:]
    if not first:
        rest = rest[1:]
    if last:
        outs, totals, held, sem = rest[:-3], rest[-3], rest[-2], rest[-1]
    else:
        totals, held, sem = rest
    copies = []
    start = 0
    for index, piece in enumerate(pieces):
        spot = held.at[pl.ds(start, piece.shape[0])]
        copies.append(pltpu.make_async_copy(piece, spot, sem.at[index]))
        copies[-1].start()
        start += piece.shape[0]
    if first:
        totals[...] = jnp.zeros_like(totals)
    for copy in copies:
        copy.wait()

    def add(g, carry):
        sums = []
        for u in range(UNROLL):
            index = g * UNROLL + u
            product = jnp.dot(
                values[order[group, 0, index]],
                held[order[group, 2, index]],
                preferred_element_type=jnp.float32,
            )
            sums.append((order[group, 1, index], product))
        for row, product in sums:
            totals[row] += product
        return carry

    lax.fori_loop(0, order[group, 3, 0], add, 0)
    if last:
        members = len(outs) // CHUNKS
        size = outs[0].shape[0]
        for index, out in enumerate(outs):
            chunk, turn = index // members, index % members
            begin = (chunk * members + (member[0] ^ turn)) * size
            for tile in range(size):
                out[tile] = totals[begin + tile].astype(out.dtype)


def add_group(group, row_tiles, order, member, values, pieces, totals):
    tile = values.shape[-1]
    pieces = [piece.reshape(-1, tile, piece.shape[-1]) for piece in pieces]
    width = pieces[0].shape[-1]
    room = sum(piece.shape[0] for piece in pieces)
    first, last = group == 0, group == 2
    vmem = pl.BlockSpec(memory_space=pltpu.VMEM)
    smem = pl.BlockSpec(memory_space=pltpu.SMEM)
    any_space = pl.BlockSpec(memory_space=pl.ANY)
    operands = [order, member, values, *pieces] + ([] if first else [totals])
    specs = [smem, smem, vmem] + [any_space] * len(pieces) + ([] if first else [vmem])
    total = jax.ShapeDtypeStruct((row_tiles + 1, tile, width), jnp.float32)
    shapes = [total]
    if last:
        size = row_tiles // (4 * CHUNKS)
        shapes = [jax.ShapeDtypeStruct((size, tile, width), jnp.bfloat16)] * (4 * CHUNKS) + [total]
    return pl.pallas_call(
        functools.partial(add_kernel, group, first, last, len(pieces)),
        out_shape=tuple(shapes),
        in_specs=specs,
        out_specs=(vmem,) * len(shapes),
        scratch_shapes=[
            pltpu.VMEM((room, tile, width), jnp.bfloat16),
            pltpu.SemaphoreType.DMA((len(pieces),)),
        ],
        input_output_aliases={} if first else {len(operands) - 1: len(shapes) - 1},
        compiler_params=pltpu.CompilerParams(vmem_limit_bytes=24 << 20),
        cost_estimate=pl.CostEstimate(flops=1000, bytes_accessed=1000, transcendentals=0),
        name="add_tiles",
    )(*operands)


def mix_kernel(member, *rest):
    members = 4
    pieces, weight, bias, outs = rest[:members], rest[members], rest[members + 1], rest[members + 2 :]
    me = member[0]
    width = pieces[0].shape[1]
    left = jnp.concatenate([piece[...] for piece in pieces], axis=1)
    for turn, out in enumerate(outs):
        col = pl.multiple_of((me ^ turn) * width, width)
        right = jnp.concatenate(
            [
                weight[pl.ds(pl.multiple_of((me ^ other) * width, width), width), pl.ds(col, width)]
                for other in range(members)
            ],
            axis=0,
        )
        total = jnp.dot(left, right, preferred_element_type=jnp.float32)
        total = total + bias[turn : turn + 1]
        out[...] = jnp.maximum(total, 0.0).astype(out.dtype)


def mix(member, pieces, weight, bias):
    shape = jax.ShapeDtypeStruct(pieces[0].shape, pieces[0].dtype)
    vmem = pl.BlockSpec(memory_space=pltpu.VMEM)
    return pl.pallas_call(
        mix_kernel,
        out_shape=(shape,) * 4,
        in_specs=[pl.BlockSpec(memory_space=pltpu.SMEM)] + [vmem] * 6,
        out_specs=(vmem,) * 4,
        compiler_params=pltpu.CompilerParams(vmem_limit_bytes=16 << 20),
        cost_estimate=pl.CostEstimate(flops=1000, bytes_accessed=1000, transcendentals=0),
        name="mix",
    )(member, *pieces, weight, bias)


def join_kernel(member, *rest):
    pieces, out = rest[:-1], rest[-1]
    for index, piece in enumerate(pieces):
        size = piece.shape[0]
        begin = ((index // 4) * 4 + (member[0] ^ (index % 4))) * size
        out[pl.ds(pl.multiple_of(begin, size), size)] = piece[...]


def join(member, pieces):
    rows = sum(piece.shape[0] for piece in pieces)
    vmem = pl.BlockSpec(memory_space=pltpu.VMEM)
    return pl.pallas_call(
        join_kernel,
        out_shape=jax.ShapeDtypeStruct((rows, pieces[0].shape[1]), pieces[0].dtype),
        in_specs=[pl.BlockSpec(memory_space=pltpu.SMEM)] + [vmem] * len(pieces),
        out_specs=vmem,
        compiler_params=pltpu.CompilerParams(vmem_limit_bytes=16 << 20),
        cost_estimate=pl.CostEstimate(flops=1000, bytes_accessed=1000, transcendentals=0),
        name="join",
    )(member, *pieces)


def body(features, tile_values, tile_rows, tile_cols, tile_counts, weight, bias):
    row_count, width = features.shape
    tile = tile_values.shape[-1]
    row_tiles = row_count // tile
    half = row_count // 2
    member = lax.axis_index("feat").reshape(1).astype(jnp.int32)
    place = lax.axis_index("blk").reshape(1).astype(jnp.int32)
    order = plan(row_tiles, tile_rows, tile_cols, tile_counts, place)
    sibling = flipped(features, "blk", 1)
    beside = flipped(features, "blk", 2)
    above = flipped(features, "blk", 4)
    (totals,) = add_group(0, row_tiles, order, member, tile_values, [features, sibling], None)
    own_bias, totals = tie(bias[None], totals)
    biases = [flipped(own_bias, "feat", turn) for turn in (1, 2, 3)]
    beside, above, *biases = tie(beside, above, *biases)
    biases = [own_bias, *biases]
    corner = [flipped(above[:half], "blk", 2), flipped(beside[half:], "blk", 4)]
    near = [beside, above, flipped(beside, "blk", 1), flipped(above, "blk", 1)]
    (totals,) = add_group(1, row_tiles, order, member, tile_values, near, totals)
    *corner, totals = tie(*corner, totals)
    corner += [flipped(piece, "blk", 1) for piece in corner]
    *parts, totals = add_group(2, row_tiles, order, member, tile_values, corner, totals)
    every_bias = jnp.concatenate(biases)
    parts = [part.reshape(-1, width) for part in parts]
    done = []
    for chunk in range(CHUNKS):
        own = parts[4 * chunk : 4 * chunk + 4]
        came = {turn: flipped(own[turn], "feat", turn) for turn in TURNS}
        outs = mix(member, [own[0], came[1], came[2], came[3]], weight, every_bias)
        came = {turn: flipped(outs[turn], "feat", turn) for turn in TURNS}
        done += [outs[0], came[1], came[2], came[3]]
    return join(member, done)


def solution(mesh):
    in_specs = (
        P("blk", "feat"),
        P("blk", None, None),
        P("blk"),
        P("blk"),
        P("blk"),
        P(),
        P("feat"),
    )
    out_specs = P("blk", "feat")
    chosen = body if mesh.shape["blk"] == 8 and mesh.shape["feat"] == 4 else ring_body
    return jax.shard_map(chosen, mesh=mesh, in_specs=in_specs, out_specs=out_specs, check_vma=False)
```

```python
import functools

import jax
import jax.numpy as jnp
import numpy as np
from jax import lax
from jax.experimental import pallas as pl
from jax.experimental.pallas import tpu as pltpu
from jax.sharding import PartitionSpec as P

CHUNKS = 2
UNROLL = 16
TURNS = (2, 3, 1)


def shifted(shard, axis, by):
    count = lax.axis_size(axis)
    return lax.ppermute(shard, axis, [(i, (i + by) % count) for i in range(count)])


def flipped(shard, axis, bits):
    count = lax.axis_size(axis)
    return lax.ppermute(shard, axis, [(i, i ^ bits) for i in range(count)])


def pick_tiles(current, wanted, row_tiles, tile_size):
    source = current.reshape(row_tiles, tile_size, current.shape[-1])
    return jnp.take(source, wanted, axis=0)


def add_tiles(totals, picked, offset, values_all, row_ids, tile_counts):
    row_tiles = totals.shape[0]
    slot_count = row_ids.shape[1]
    products = jnp.einsum(
        "ktj,kjf->ktf", values_all[offset], picked, preferred_element_type=jnp.float32
    )
    active = jnp.arange(slot_count) < tile_counts[offset]
    one_hot = (
        (row_ids[offset][None, :] == jnp.arange(row_tiles)[:, None]) & active[None, :]
    ).astype(jnp.float32)
    return totals + jnp.einsum("rk,ktf->rtf", one_hot, products, precision=lax.Precision.HIGHEST)


def ring_body(features, tile_values, tile_rows, tile_cols, tile_counts, weight, bias):
    row_count, col_width = features.shape
    tile_size = tile_values.shape[-1]
    row_tiles = row_count // tile_size
    steps_all = tile_counts.shape[0]
    slot_count = tile_rows.shape[0] // steps_all
    values_all = tile_values.reshape(steps_all, slot_count, tile_size, tile_size)
    row_ids = tile_rows.reshape(steps_all, slot_count)
    col_ids = tile_cols.reshape(steps_all, slot_count)
    totals = jnp.zeros((row_tiles, tile_size, col_width), jnp.float32)
    own_picked = pick_tiles(features, col_ids[0], row_tiles, tile_size)
    totals = add_tiles(totals, own_picked, 0, values_all, row_ids, tile_counts)
    current = features
    for offset in range(1, steps_all):
        current = shifted(current, "blk", 1)
        picked = pick_tiles(current, col_ids[offset], row_tiles, tile_size)
        totals = add_tiles(totals, picked, offset, values_all, row_ids, tile_counts)
    aggregate = totals.reshape(row_count, col_width).astype(jnp.bfloat16)
    out_width = bias.shape[0]
    member = lax.axis_index("feat")
    own_cols = lax.dynamic_slice_in_dim(weight, member * out_width, out_width, 1)
    mixed = jnp.dot(
        lax.all_gather(aggregate, "feat", axis=1, tiled=True),
        own_cols,
        preferred_element_type=jnp.float32,
    )
    return jnp.maximum(mixed + bias[None, :], 0.0).astype(jnp.bfloat16)


def tie(*arrays):
    return lax.optimization_barrier(arrays)


def spots(row_tiles):
    table = np.zeros((8, row_tiles), np.int32)
    for away in range(8):
        side, way = away & 1, away >> 1
        group = (0, 1, 1, 2 + side)[way]
        start = (side, 2 * side, 2 * side + 1, 0)[way] * row_tiles
        table[away] = group * 1024 + start + np.arange(row_tiles)
    return table.reshape(-1)


def plan_kernel(row_tiles, rows, cols, counts, place, table, order, found):
    steps = counts.shape[0]
    slots = rows.shape[0] // steps
    where = place[0]
    for group in range(4):
        found[group] = 0

    def offset_loop(offset, carry):
        away = where ^ ((where + steps - offset) & (steps - 1))

        def slot_loop(k, carry):
            slot = offset * slots + k
            key = table[away * row_tiles + cols[slot]]
            group = key >> 10
            at = found[group]
            order[group, 0, at] = slot
            order[group, 1, at] = rows[slot]
            order[group, 2, at] = key & 1023
            found[group] = at + 1
            return carry

        return lax.fori_loop(0, counts[offset], slot_loop, carry)

    lax.fori_loop(0, steps, offset_loop, 0)
    for group in range(4):
        at = found[group]
        for u in range(UNROLL):
            order[group, 0, at + u] = 0
            order[group, 1, at + u] = row_tiles
            order[group, 2, at + u] = 0
        order[group, 3, 0] = (at + UNROLL - 1) // UNROLL


def plan(row_tiles, rows, cols, counts, place):
    room = rows.shape[0] + UNROLL
    return pl.pallas_call(
        functools.partial(plan_kernel, row_tiles),
        out_shape=jax.ShapeDtypeStruct((4, 4, room), jnp.int32),
        in_specs=[pl.BlockSpec(memory_space=pltpu.SMEM)] * 5,
        out_specs=pl.BlockSpec(memory_space=pltpu.SMEM),
        scratch_shapes=[pltpu.SMEM((4,), jnp.int32)],
        cost_estimate=pl.CostEstimate(flops=10**9, bytes_accessed=1000, transcendentals=0),
        name="plan",
    )(rows, cols, counts, place, jnp.asarray(spots(row_tiles)))


def add_kernel(group, first, last, count, order, member, values, *rest):
    pieces, rest = rest[:count], rest[count:]
    if not first:
        rest = rest[1:]
    if last:
        outs, totals, held, sem = rest[:-3], rest[-3], rest[-2], rest[-1]
    else:
        totals, held, sem = rest
    copies = []
    start = 0
    for index, piece in enumerate(pieces):
        spot = held.at[pl.ds(start, piece.shape[0])]
        copies.append(pltpu.make_async_copy(piece, spot, sem.at[index]))
        copies[-1].start()
        start += piece.shape[0]
    if first:
        totals[...] = jnp.zeros_like(totals)
    for copy in copies:
        copy.wait()

    def add(g, carry):
        sums = []
        for u in range(UNROLL):
            index = g * UNROLL + u
            product = jnp.dot(
                values[order[group, 0, index]],
                held[order[group, 2, index]],
                preferred_element_type=jnp.float32,
            )
            sums.append((order[group, 1, index], product))
        for row, product in sums:
            totals[row] += product
        return carry

    lax.fori_loop(0, order[group, 3, 0], add, 0)
    if last:
        members = len(outs) // CHUNKS
        size = outs[0].shape[0]
        for index, out in enumerate(outs):
            chunk, turn = index // members, index % members
            begin = (chunk * members + (member[0] ^ turn)) * size
            for tile in range(size):
                out[tile] = totals[begin + tile].astype(out.dtype)


def add_group(group, row_tiles, order, member, values, pieces, totals):
    tile = values.shape[-1]
    pieces = [piece.reshape(-1, tile, piece.shape[-1]) for piece in pieces]
    width = pieces[0].shape[-1]
    room = sum(piece.shape[0] for piece in pieces)
    first, last = group == 0, group == 3
    vmem = pl.BlockSpec(memory_space=pltpu.VMEM)
    smem = pl.BlockSpec(memory_space=pltpu.SMEM)
    any_space = pl.BlockSpec(memory_space=pl.ANY)
    operands = [order, member, values, *pieces] + ([] if first else [totals])
    specs = [smem, smem, vmem] + [any_space] * len(pieces) + ([] if first else [vmem])
    total = jax.ShapeDtypeStruct((row_tiles + 1, tile, width), jnp.float32)
    shapes = [total]
    if last:
        size = row_tiles // (4 * CHUNKS)
        shapes = [jax.ShapeDtypeStruct((size, tile, width), jnp.bfloat16)] * (4 * CHUNKS) + [total]
    return pl.pallas_call(
        functools.partial(add_kernel, group, first, last, len(pieces)),
        out_shape=tuple(shapes),
        in_specs=specs,
        out_specs=(vmem,) * len(shapes),
        scratch_shapes=[
            pltpu.VMEM((room, tile, width), jnp.bfloat16),
            pltpu.SemaphoreType.DMA((len(pieces),)),
        ],
        input_output_aliases={} if first else {len(operands) - 1: len(shapes) - 1},
        compiler_params=pltpu.CompilerParams(vmem_limit_bytes=24 << 20),
        cost_estimate=pl.CostEstimate(flops=10**9, bytes_accessed=1000, transcendentals=0),
        name="add_tiles",
    )(*operands)


def mix_kernel(member, *rest):
    members = 4
    pieces, weight, bias, outs = rest[:members], rest[members], rest[members + 1], rest[members + 2 :]
    me = member[0]
    width = pieces[0].shape[1]
    left = jnp.concatenate([piece[...] for piece in pieces], axis=1)
    for turn, out in enumerate(outs):
        col = pl.multiple_of((me ^ turn) * width, width)
        right = jnp.concatenate(
            [
                weight[pl.ds(pl.multiple_of((me ^ other) * width, width), width), pl.ds(col, width)]
                for other in range(members)
            ],
            axis=0,
        )
        total = jnp.dot(left, right, preferred_element_type=jnp.float32)
        total = total + bias[turn : turn + 1]
        out[...] = jnp.maximum(total, 0.0).astype(out.dtype)


def mix(member, pieces, weight, bias):
    shape = jax.ShapeDtypeStruct(pieces[0].shape, pieces[0].dtype)
    vmem = pl.BlockSpec(memory_space=pltpu.VMEM)
    return pl.pallas_call(
        mix_kernel,
        out_shape=(shape,) * 4,
        in_specs=[pl.BlockSpec(memory_space=pltpu.SMEM)] + [vmem] * 6,
        out_specs=(vmem,) * 4,
        compiler_params=pltpu.CompilerParams(vmem_limit_bytes=16 << 20),
        cost_estimate=pl.CostEstimate(flops=1000, bytes_accessed=1000, transcendentals=0),
        name="mix",
    )(member, *pieces, weight, bias)


def join_kernel(member, *rest):
    pieces, out = rest[:-1], rest[-1]
    for index, piece in enumerate(pieces):
        size = piece.shape[0]
        begin = ((index // 4) * 4 + (member[0] ^ (index % 4))) * size
        out[pl.ds(pl.multiple_of(begin, size), size)] = piece[...]


def join(member, pieces):
    rows = sum(piece.shape[0] for piece in pieces)
    vmem = pl.BlockSpec(memory_space=pltpu.VMEM)
    return pl.pallas_call(
        join_kernel,
        out_shape=jax.ShapeDtypeStruct((rows, pieces[0].shape[1]), pieces[0].dtype),
        in_specs=[pl.BlockSpec(memory_space=pltpu.SMEM)] + [vmem] * len(pieces),
        out_specs=vmem,
        compiler_params=pltpu.CompilerParams(vmem_limit_bytes=16 << 20),
        cost_estimate=pl.CostEstimate(flops=1000, bytes_accessed=1000, transcendentals=0),
        name="join",
    )(member, *pieces)


def body(features, tile_values, tile_rows, tile_cols, tile_counts, weight, bias):
    row_count, width = features.shape
    tile = tile_values.shape[-1]
    row_tiles = row_count // tile
    half = row_count // 2
    member = lax.axis_index("feat").reshape(1).astype(jnp.int32)
    place = lax.axis_index("blk").reshape(1).astype(jnp.int32)
    order = plan(row_tiles, tile_rows, tile_cols, tile_counts, place)
    sibling = flipped(features, "blk", 1)
    beside = flipped(features, "blk", 2)
    above = flipped(features, "blk", 4)
    (totals,) = add_group(0, row_tiles, order, member, tile_values, [features, sibling], None)
    own_bias, totals = tie(bias[None], totals)
    biases = [flipped(own_bias, "feat", turn) for turn in (1, 2, 3)]
    beside, above, *biases = tie(beside, above, *biases)
    biases = [own_bias, *biases]
    corner = [flipped(above[:half], "blk", 2), flipped(beside[half:], "blk", 4)]
    near = [beside, above, flipped(beside, "blk", 1), flipped(above, "blk", 1)]
    (totals,) = add_group(1, row_tiles, order, member, tile_values, near, totals)
    *corner, totals = tie(*corner, totals)
    (totals,) = add_group(2, row_tiles, order, member, tile_values, corner, totals)
    corner = [flipped(piece, "blk", 1) for piece in corner]
    *parts, totals = add_group(3, row_tiles, order, member, tile_values, corner, totals)
    every_bias = jnp.concatenate(biases)
    parts = [part.reshape(-1, width) for part in parts]
    done = []
    for chunk in range(CHUNKS):
        own = parts[4 * chunk : 4 * chunk + 4]
        came = {turn: flipped(own[turn], "feat", turn) for turn in TURNS}
        outs = mix(member, [own[0], came[1], came[2], came[3]], weight, every_bias)
        came = {turn: flipped(outs[turn], "feat", turn) for turn in TURNS}
        done += [outs[0], came[1], came[2], came[3]]
    return join(member, done)


def solution(mesh):
    in_specs = (
        P("blk", "feat"),
        P("blk", None, None),
        P("blk"),
        P("blk"),
        P("blk"),
        P(),
        P("feat"),
    )
    out_specs = P("blk", "feat")
    chosen = body if mesh.shape["blk"] == 8 and mesh.shape["feat"] == 4 else ring_body
    return jax.shard_map(chosen, mesh=mesh, in_specs=in_specs, out_specs=out_specs, check_vma=False)
```

```python
import functools

import jax
import jax.numpy as jnp
import numpy as np
from jax import lax
from jax.experimental import pallas as pl
from jax.experimental.pallas import tpu as pltpu
from jax.sharding import PartitionSpec as P

CHUNKS = 2
UNROLL = 16
TURNS = (2, 3, 1)


def shifted(shard, axis, by):
    count = lax.axis_size(axis)
    return lax.ppermute(shard, axis, [(i, (i + by) % count) for i in range(count)])


def flipped(shard, axis, bits):
    count = lax.axis_size(axis)
    return lax.ppermute(shard, axis, [(i, i ^ bits) for i in range(count)])


def pick_tiles(current, wanted, row_tiles, tile_size):
    source = current.reshape(row_tiles, tile_size, current.shape[-1])
    return jnp.take(source, wanted, axis=0)


def add_tiles(totals, picked, offset, values_all, row_ids, tile_counts):
    row_tiles = totals.shape[0]
    slot_count = row_ids.shape[1]
    products = jnp.einsum(
        "ktj,kjf->ktf", values_all[offset], picked, preferred_element_type=jnp.float32
    )
    active = jnp.arange(slot_count) < tile_counts[offset]
    one_hot = (
        (row_ids[offset][None, :] == jnp.arange(row_tiles)[:, None]) & active[None, :]
    ).astype(jnp.float32)
    return totals + jnp.einsum("rk,ktf->rtf", one_hot, products, precision=lax.Precision.HIGHEST)


def ring_body(features, tile_values, tile_rows, tile_cols, tile_counts, weight, bias):
    row_count, col_width = features.shape
    tile_size = tile_values.shape[-1]
    row_tiles = row_count // tile_size
    steps_all = tile_counts.shape[0]
    slot_count = tile_rows.shape[0] // steps_all
    values_all = tile_values.reshape(steps_all, slot_count, tile_size, tile_size)
    row_ids = tile_rows.reshape(steps_all, slot_count)
    col_ids = tile_cols.reshape(steps_all, slot_count)
    totals = jnp.zeros((row_tiles, tile_size, col_width), jnp.float32)
    own_picked = pick_tiles(features, col_ids[0], row_tiles, tile_size)
    totals = add_tiles(totals, own_picked, 0, values_all, row_ids, tile_counts)
    current = features
    for offset in range(1, steps_all):
        current = shifted(current, "blk", 1)
        picked = pick_tiles(current, col_ids[offset], row_tiles, tile_size)
        totals = add_tiles(totals, picked, offset, values_all, row_ids, tile_counts)
    aggregate = totals.reshape(row_count, col_width).astype(jnp.bfloat16)
    out_width = bias.shape[0]
    member = lax.axis_index("feat")
    own_cols = lax.dynamic_slice_in_dim(weight, member * out_width, out_width, 1)
    mixed = jnp.dot(
        lax.all_gather(aggregate, "feat", axis=1, tiled=True),
        own_cols,
        preferred_element_type=jnp.float32,
    )
    return jnp.maximum(mixed + bias[None, :], 0.0).astype(jnp.bfloat16)


def tie(*arrays):
    return lax.optimization_barrier(arrays)


def spots(row_tiles):
    table = np.zeros((8, row_tiles), np.int32)
    for away in range(8):
        side, way = away & 1, away >> 1
        group = (0, 1, 1, 2 + side)[way]
        start = (side, 2 * side, 2 * side + 1, 0)[way] * row_tiles
        table[away] = group * 1024 + start + np.arange(row_tiles)
    return table.reshape(-1)


def plan_kernel(row_tiles, rows, cols, counts, place, table, order, found):
    steps = counts.shape[0]
    slots = rows.shape[0] // steps
    where = place[0]
    for group in range(4):
        found[group] = 0

    def offset_loop(offset, carry):
        away = where ^ ((where + steps - offset) & (steps - 1))

        def slot_loop(k, carry):
            slot = offset * slots + k
            key = table[away * row_tiles + cols[slot]]
            group = key >> 10
            at = found[group]
            order[group, 0, at] = slot
            order[group, 1, at] = rows[slot]
            order[group, 2, at] = key & 1023
            found[group] = at + 1
            return carry

        return lax.fori_loop(0, counts[offset], slot_loop, carry)

    lax.fori_loop(0, steps, offset_loop, 0)
    for group in range(4):
        at = found[group]
        for u in range(UNROLL):
            order[group, 0, at + u] = 0
            order[group, 1, at + u] = row_tiles
            order[group, 2, at + u] = 0
        order[group, 3, 0] = (at + UNROLL - 1) // UNROLL


def plan(row_tiles, rows, cols, counts, place):
    room = rows.shape[0] + UNROLL
    return pl.pallas_call(
        functools.partial(plan_kernel, row_tiles),
        out_shape=jax.ShapeDtypeStruct((4, 4, room), jnp.int32),
        in_specs=[pl.BlockSpec(memory_space=pltpu.SMEM)] * 5,
        out_specs=pl.BlockSpec(memory_space=pltpu.SMEM),
        scratch_shapes=[pltpu.SMEM((4,), jnp.int32)],
        cost_estimate=pl.CostEstimate(flops=10**9, bytes_accessed=1000, transcendentals=0),
        name="plan",
    )(rows, cols, counts, place, jnp.asarray(spots(row_tiles)))


def add_kernel(group, first, last, count, order, member, values, *rest):
    pieces, rest = rest[:count], rest[count:]
    if not first:
        rest = rest[1:]
    if last:
        outs, totals, held, sem = rest[:-3], rest[-3], rest[-2], rest[-1]
    else:
        totals, held, sem = rest
    copies = []
    start = 0
    for index, piece in enumerate(pieces):
        spot = held.at[pl.ds(start, piece.shape[0])]
        copies.append(pltpu.make_async_copy(piece, spot, sem.at[index]))
        copies[-1].start()
        start += piece.shape[0]
    if first:
        totals[...] = jnp.zeros_like(totals)
    for copy in copies:
        copy.wait()

    def add(g, carry):
        sums = []
        for u in range(UNROLL):
            index = g * UNROLL + u
            product = jnp.dot(
                values[order[group, 0, index]],
                held[order[group, 2, index]],
                preferred_element_type=jnp.float32,
            )
            sums.append((order[group, 1, index], product))
        for row, product in sums:
            totals[row] += product
        return carry

    lax.fori_loop(0, order[group, 3, 0], add, 0)
    if last:
        members = len(outs) // CHUNKS
        size = outs[0].shape[0]
        for index, out in enumerate(outs):
            chunk, turn = index // members, index % members
            begin = (chunk * members + (member[0] ^ turn)) * size
            for tile in range(size):
                out[tile] = totals[begin + tile].astype(out.dtype)


def add_group(group, row_tiles, order, member, values, pieces, totals):
    tile = values.shape[-1]
    pieces = [piece.reshape(-1, tile, piece.shape[-1]) for piece in pieces]
    width = pieces[0].shape[-1]
    room = sum(piece.shape[0] for piece in pieces)
    first, last = group == 0, group == 3
    vmem = pl.BlockSpec(memory_space=pltpu.VMEM)
    smem = pl.BlockSpec(memory_space=pltpu.SMEM)
    any_space = pl.BlockSpec(memory_space=pl.ANY)
    operands = [order, member, values, *pieces] + ([] if first else [totals])
    specs = [smem, smem, vmem] + [any_space] * len(pieces) + ([] if first else [vmem])
    total = jax.ShapeDtypeStruct((row_tiles + 1, tile, width), jnp.float32)
    shapes = [total]
    if last:
        size = row_tiles // (4 * CHUNKS)
        shapes = [jax.ShapeDtypeStruct((size, tile, width), jnp.bfloat16)] * (4 * CHUNKS) + [total]
    return pl.pallas_call(
        functools.partial(add_kernel, group, first, last, len(pieces)),
        out_shape=tuple(shapes),
        in_specs=specs,
        out_specs=(vmem,) * len(shapes),
        scratch_shapes=[
            pltpu.VMEM((room, tile, width), jnp.bfloat16),
            pltpu.SemaphoreType.DMA((len(pieces),)),
        ],
        input_output_aliases={} if first else {len(operands) - 1: len(shapes) - 1},
        compiler_params=pltpu.CompilerParams(vmem_limit_bytes=24 << 20),
        cost_estimate=pl.CostEstimate(flops=10**9, bytes_accessed=1000, transcendentals=0),
        name="add_tiles",
    )(*operands)


def mix_kernel(member, *rest):
    members = 4
    pieces, weight, bias, outs = rest[:members], rest[members], rest[members + 1], rest[members + 2 :]
    me = member[0]
    width = pieces[0].shape[1]
    left = jnp.concatenate([piece[...] for piece in pieces], axis=1)
    for turn, out in enumerate(outs):
        col = pl.multiple_of((me ^ turn) * width, width)
        right = jnp.concatenate(
            [
                weight[pl.ds(pl.multiple_of((me ^ other) * width, width), width), pl.ds(col, width)]
                for other in range(members)
            ],
            axis=0,
        )
        total = jnp.dot(left, right, preferred_element_type=jnp.float32)
        total = total + bias[turn : turn + 1]
        out[...] = jnp.maximum(total, 0.0).astype(out.dtype)


def mix(member, pieces, weight, bias):
    shape = jax.ShapeDtypeStruct(pieces[0].shape, pieces[0].dtype)
    vmem = pl.BlockSpec(memory_space=pltpu.VMEM)
    return pl.pallas_call(
        mix_kernel,
        out_shape=(shape,) * 4,
        in_specs=[pl.BlockSpec(memory_space=pltpu.SMEM)] + [vmem] * 6,
        out_specs=(vmem,) * 4,
        compiler_params=pltpu.CompilerParams(vmem_limit_bytes=16 << 20),
        cost_estimate=pl.CostEstimate(flops=1000, bytes_accessed=1000, transcendentals=0),
        name="mix",
    )(member, *pieces, weight, bias)


def join_kernel(member, *rest):
    pieces, out = rest[:-1], rest[-1]
    for index, piece in enumerate(pieces):
        size = piece.shape[0]
        begin = ((index // 4) * 4 + (member[0] ^ (index % 4))) * size
        out[pl.ds(pl.multiple_of(begin, size), size)] = piece[...]


def join(member, pieces):
    rows = sum(piece.shape[0] for piece in pieces)
    vmem = pl.BlockSpec(memory_space=pltpu.VMEM)
    return pl.pallas_call(
        join_kernel,
        out_shape=jax.ShapeDtypeStruct((rows, pieces[0].shape[1]), pieces[0].dtype),
        in_specs=[pl.BlockSpec(memory_space=pltpu.SMEM)] + [vmem] * len(pieces),
        out_specs=vmem,
        compiler_params=pltpu.CompilerParams(vmem_limit_bytes=16 << 20),
        cost_estimate=pl.CostEstimate(flops=1000, bytes_accessed=1000, transcendentals=0),
        name="join",
    )(member, *pieces)


def body(features, tile_values, tile_rows, tile_cols, tile_counts, weight, bias):
    row_count, width = features.shape
    tile = tile_values.shape[-1]
    row_tiles = row_count // tile
    half = row_count // 2
    member = lax.axis_index("feat").reshape(1).astype(jnp.int32)
    place = lax.axis_index("blk").reshape(1).astype(jnp.int32)
    order = plan(row_tiles, tile_rows, tile_cols, tile_counts, place)
    sibling = flipped(features, "blk", 1)
    beside = flipped(features, "blk", 2)
    above = flipped(features, "blk", 4)
    (totals,) = add_group(0, row_tiles, order, member, tile_values, [features, sibling], None)
    own_bias, totals = tie(bias[None], totals)
    biases = [flipped(own_bias, "feat", turn) for turn in (1, 2, 3)]
    beside, above, *biases = tie(beside, above, *biases)
    biases = [own_bias, *biases]
    low, high = above[:half], beside[half:]
    beside, above, low, high = tie(beside, above, low, high)
    corner = [flipped(low, "blk", 2), flipped(high, "blk", 4)]
    near = [beside, above, flipped(beside, "blk", 1), flipped(above, "blk", 1)]
    (totals,) = add_group(1, row_tiles, order, member, tile_values, near, totals)
    *corner, totals = tie(*corner, totals)
    (totals,) = add_group(2, row_tiles, order, member, tile_values, corner, totals)
    corner = [flipped(piece, "blk", 1) for piece in corner]
    *parts, totals = add_group(3, row_tiles, order, member, tile_values, corner, totals)
    every_bias = jnp.concatenate(biases)
    parts = [part.reshape(-1, width) for part in parts]
    done = []
    for chunk in range(CHUNKS):
        own = parts[4 * chunk : 4 * chunk + 4]
        came = {turn: flipped(own[turn], "feat", turn) for turn in TURNS}
        outs = mix(member, [own[0], came[1], came[2], came[3]], weight, every_bias)
        came = {turn: flipped(outs[turn], "feat", turn) for turn in TURNS}
        done += [outs[0], came[1], came[2], came[3]]
    return join(member, done)


def solution(mesh):
    in_specs = (
        P("blk", "feat"),
        P("blk", None, None),
        P("blk"),
        P("blk"),
        P("blk"),
        P(),
        P("feat"),
    )
    out_specs = P("blk", "feat")
    chosen = body if mesh.shape["blk"] == 8 and mesh.shape["feat"] == 4 else ring_body
    return jax.shard_map(chosen, mesh=mesh, in_specs=in_specs, out_specs=out_specs, check_vma=False)
```
